32 devices in a mesh: rows: 32 (over z, y, x, core).
Axes of the slice: x: 2, y: 2, z: 4, core: 2. Of those that a mesh axis runs over, the one named last changes fastest.
Arguments:
- diag_noise: bfloat16 [448, 128, 128], P('rows'), may hold values from -1 to 1
- couplings: bfloat16 [448, 3, 128, 128], P('rows'), may hold values from -1 to 1
- shifts: bfloat16 [448, 128], P('rows'), may hold values from 1.5 to 3
- near_devices: int32 [448, 3], P('rows'), may hold values from 0 to 30, all different within a row; in each aligned block of 14 rows (0 to 13, 14 to 27, ...) at most 3 rows name the same one
- near_slots: int32 [448, 3], P('rows'), may hold values from 0 to 13
- vectors: float32 [32, 57344], P(None, 'rows'), may hold values from -6 to 6
Outputs:
- transformed: float32 [32, 57344], P(None, 'rows')
The draws below stay inside these ranges and needn't reach their ends.
Inputs may be any that keep to these rules, and one draw needn't show every extreme that they name: `near_devices`: each row names three different distances. Among the 14 block rows of one device, no distance is named by more than 3 rows, and in some such group one distance is named by exactly 3 rows.
All inputs are finite; a program needn't handle non-finite values.
Results may differ from the reference program's by a relative error of at most 0.0014.
Values may be sent and summed in bfloat16 or wider, within the bound.
A program may use at most 128 MiB of HBM per device.

```python
import math
import jax
import jax.numpy as jnp
import numpy as np
from jax import lax

BLK = 128
NVEC = 32
RB = 14
NB = 448
PEERS = 31
CAP = 3
N_ROWS = 32


def random_signs(key, shape):
    return jnp.where(jax.random.bernoulli(key, 0.5, shape), 1.0, -1.0).astype(jnp.float32)


def draw_diag_noise(key, part):
    values = jax.random.uniform(jax.random.fold_in(key, 101), (NB, BLK, BLK), jnp.float32, -1.0, 1.0)
    signs = random_signs(jax.random.fold_in(key, 103), (NB, BLK))
    shared = signs[:, :, None] * signs[:, None, :]
    values = 0.25 * shared + 0.75 * values
    return values.astype(jnp.bfloat16)


def draw_couplings(key, part):
    values = jax.random.uniform(jax.random.fold_in(key, 201), (NB, 3, BLK, BLK), jnp.float32, -1.0, 1.0)
    row_signs = random_signs(jax.random.fold_in(key, 203), (NB, 1, BLK))
    col_signs = random_signs(jax.random.fold_in(key, 204), (NB, 3, BLK))
    shared = row_signs[:, :, :, None] * col_signs[:, :, None, :]
    values = 0.15 * shared + 0.85 * values
    return values.astype(jnp.bfloat16)


def set_ends(values, key, smallest, high):
    longest = values.shape.index(max(values.shape))
    spots = []
    for shift in (0, 1):
        where = [jax.random.randint(jax.random.fold_in(key, axis), (), 0, length) for axis, length in enumerate(values.shape)]
        where[longest] = (where[longest] + shift) % values.shape[longest]
        spots.append(tuple(where))
    return values.at[spots[0]].set(smallest).at[spots[1]].set(high)


def block_scale(key, dims, split, low, high):
    def one(dim, blocks):
        steps = jax.random.uniform(jax.random.fold_in(jax.random.fold_in(key, 6), dim), (blocks,), jnp.float32, low / len(split), high / len(split))
        return jnp.repeat(jnp.exp(steps), dims[dim] // blocks).reshape((-1,) + (1,) * (len(dims) - dim - 1))

    loudness = one(*split[0])
    for cut in split[1:]:
        loudness = loudness * one(*cut)
    return loudness


def shared_out(stream_key, own, number, rows, number_of, top, reach, slope):
    ranking = jax.random.permutation(stream_key, number_of)
    crowded, ordinary = load_shares(number_of, rows * top, reach, slope, True), load_shares(number_of, rows * top, reach, slope, False)
    places = jnp.arange(number_of)

    def named(tallies, offset_by):
        used = int((tallies > 0).sum())
        fixed = max(1, used // 4)
        passed = fixed + (places - fixed + offset_by * (used - fixed)) % max(1, number_of - fixed)
        return jnp.zeros((number_of,), jnp.int32).at[ranking[jnp.where(places < fixed, places, passed)]].set(jnp.asarray(tallies, jnp.int32))

    tallies = jnp.where(number % 4 == 0, named(crowded, number // 4), named(ordinary, number - number // 4 - 1))
    mixed = jax.random.permutation(jax.random.fold_in(own, 3), number_of)
    source_of, taker = mixed[0:number_of // 2 * 2:2], mixed[1:number_of // 2 * 2:2]
    slack = jnp.minimum(tallies[source_of] - 1, reach - tallies[taker]) // 2
    slack = jnp.where((source_of == ranking[0]) | (taker == ranking[0]) | (tallies[taker] == 0), 0, jnp.maximum(slack, 0))
    passed = jax.random.randint(jax.random.fold_in(own, 4), (number_of // 2,), 0, 1 << 20) % (slack + 1)
    tallies = tallies.at[source_of].add(-passed).at[taker].add(passed)
    members = jnp.searchsorted(jnp.cumsum(tallies), jnp.arange(rows * top), side="right").astype(jnp.int32)
    grid = members.reshape(top, rows).T
    grid = grid[jax.random.permutation(jax.random.fold_in(own, 1), rows)]
    offset_by = jax.random.randint(jax.random.fold_in(own, 2), (rows, 1), 0, top)
    return jnp.take_along_axis(grid, (jnp.arange(top)[None, :] + offset_by) % top, axis=1)


def load_shares(amount, total, limit, slope, full):
    portions = [(1 << 20) // math.isqrt(grade ** slope) + 1 for grade in range(1, amount + 1)]
    largest = limit if full else min(limit, max(-(-total // amount), total * portions[0] // sum(portions)))
    least = 1 if total - largest >= amount - 1 else 0
    given, spare = [largest] + [least] * (amount - 1), total - largest - least * (amount - 1)
    while spare > 0:
        movable = [i for i in range(1, amount) if given[i] < largest] or [i for i in range(1, amount) if given[i] < limit]
        whole, remaining = sum([portions[i] for i in movable]), spare
        for i in movable:
            addition = min(limit - given[i], max(1, remaining * portions[i] // whole), spare)
            given[i] = given[i] + addition
            spare = spare - addition
    return np.array(given)


def normal_values(key, extent, width, limit, shards=(), kind=jnp.bfloat16):
    values = jax.random.normal(key, extent, jnp.float32) * width
    if len(shards) > 0:
        values = block_scale(key, extent, shards, -0.22, 0.18) * values
    return jnp.clip(values, min=-limit, max=limit).astype(kind)


def setup_inputs(seed: int = 0) -> dict:
    splits = jax.random.split(jax.random.key(seed), 7)
    diag_noise = draw_diag_noise(jax.random.fold_in(splits[6], 71), 0)
    couplings = draw_couplings(jax.random.fold_in(splits[6], 71), 0)
    shifts = jnp.clip(jnp.exp(math.log(3.0) - 0.6931472 * jax.random.uniform(splits[2], (NB, BLK), jnp.float32) ** block_scale(splits[2], (NB, BLK), ((0, 32),), -0.2, 0.2)), 1.5, 3.0).astype(jnp.bfloat16)
    near_devices_keys = jax.random.split(jax.random.fold_in(splits[3], 1), NB // RB)
    near_devices_turns = jax.random.permutation(jax.random.fold_in(splits[3], 3), NB // RB)
    near_devices = jax.vmap(lambda own, number: shared_out(jax.random.fold_in(splits[3], 2), own, number, RB, PEERS, 3, CAP, 0))(near_devices_keys, near_devices_turns).reshape((NB, 3))
    near_slots = set_ends(jax.random.randint(splits[4], (NB, 3), 0, RB), jax.random.fold_in(splits[4], 1), 0, RB - 1).astype(jnp.int32)
    vectors = normal_values(splits[5], (NVEC, NB * BLK), 1.0, 6.0, ((1, 32),), jnp.float32)
    return dict(diag_noise=diag_noise, couplings=couplings, shifts=shifts, near_devices=near_devices, near_slots=near_slots, vectors=vectors)


highest = lax.Precision.HIGHEST

def invert(matrix):
    lower_factor = jnp.linalg.cholesky(matrix)
    identity = jnp.broadcast_to(jnp.eye(matrix.shape[-1], dtype=matrix.dtype), matrix.shape)
    inverse_lower = jax.scipy.linalg.solve_triangular(lower_factor, identity, lower=True)
    return jnp.einsum('...ba,...bc->...ac', inverse_lower, inverse_lower, precision=highest)

def build_diag(noise_block, shift_block, factor):
    noise_block = noise_block.astype(jnp.float32) * factor
    symmetric = (noise_block + jnp.swapaxes(noise_block, -1, -2)) * 0.5
    eye_block = jnp.eye(noise_block.shape[-1], dtype=jnp.float32)
    return symmetric + shift_block.astype(jnp.float32)[..., :, None] * eye_block

def row_factors(diag_own, coupling, inverse_near):
    product = jnp.einsum('rmab,rmbc->rmac', coupling, inverse_near, precision=highest)
    schur_block = diag_own - jnp.einsum('rmab,rmcb->rac', product, coupling, precision=highest)
    lower_factor = jnp.linalg.cholesky(invert(schur_block))
    factor_diag = jnp.swapaxes(lower_factor, -1, -2)
    factor_off = -jnp.einsum('rba,rmbc->rmac', lower_factor, product, precision=highest)
    return (factor_diag, factor_off)

def reference(diag_noise, couplings, shifts, near_devices, near_slots, vectors):
    factor = 0.5 / math.sqrt(BLK)
    coupling_factor = 0.4 / math.sqrt(BLK)
    owner_device = jnp.arange(NB, dtype=jnp.int32) // RB
    near_index = ((owner_device[:, None] - 1 - near_devices) % N_ROWS * RB + near_slots).astype(jnp.int32)
    inverse_all = invert(build_diag(diag_noise, shifts, factor))
    noise_spans = diag_noise.reshape(N_ROWS, RB, BLK, BLK)
    shift_spans = shifts.reshape(N_ROWS, RB, BLK)
    coupling_spans = couplings.reshape(N_ROWS, RB, 3, BLK, BLK)
    index_spans = near_index.reshape(N_ROWS, RB, 3)

    def setup_block(pieces):
        noise_block, shift_block, coupling_raw, index_block = pieces
        diag_own = build_diag(noise_block, shift_block, factor)
        coupling = coupling_raw.astype(jnp.float32) * coupling_factor
        return row_factors(diag_own, coupling, inverse_all[index_block])
    factor_diag, factor_off = lax.map(setup_block, (noise_spans, shift_spans, coupling_spans, index_spans))
    factor_diag = factor_diag.reshape(NB, BLK, BLK)
    factor_off = factor_off.reshape(NB, 3, BLK, BLK)
    vector_rows = vectors.reshape(NVEC, NB, BLK).transpose(1, 0, 2)
    left_product = jnp.einsum('rva,rab->rvb', vector_rows, factor_diag, precision=highest)
    outgoing = jnp.einsum('rva,rmab->rmvb', vector_rows, factor_off, precision=highest)
    left_product = left_product.at[near_index].add(outgoing)

    def coupling_block(pieces):
        noise_block, shift_block, coupling_raw, index_block, left_block = pieces
        diag_own = build_diag(noise_block, shift_block, factor)
        coupling = coupling_raw.astype(jnp.float32) * coupling_factor
        middle = jnp.einsum('rva,rab->rvb', left_block, diag_own, precision=highest)
        middle = middle + jnp.einsum('rmvb,rmab->rva', left_product[index_block], coupling, precision=highest)
        pushed = jnp.einsum('rva,rmab->rmvb', left_block, coupling, precision=highest)
        return (middle, pushed)
    middle_product, pushed = lax.map(coupling_block, (noise_spans, shift_spans, coupling_spans, index_spans, left_product.reshape(N_ROWS, RB, NVEC, BLK)))
    middle_product = middle_product.reshape(NB, NVEC, BLK).at[near_index].add(pushed.reshape(NB, 3, NVEC, BLK))
    result = jnp.einsum('rvb,rab->rva', middle_product, factor_diag, precision=highest)
    result = result + jnp.einsum('rmvb,rmab->rva', middle_product[near_index], factor_off, precision=highest)
    return result.transpose(1, 0, 2).reshape(NVEC, NB * BLK)
```

```python
import functools
import math

import jax
import jax.numpy as jnp
from jax import lax
from jax.experimental import pallas as pl
from jax.experimental.pallas import tpu as pltpu
from jax.sharding import PartitionSpec as P

highest = lax.Precision.HIGHEST
PANEL = 16


def split3(x):
    high = x.astype(jnp.bfloat16)
    rest = x - high.astype(jnp.float32)
    mid = rest.astype(jnp.bfloat16)
    low = (rest - mid.astype(jnp.float32)).astype(jnp.bfloat16)
    return high, mid, low


def tdot(a, b):
    return lax.dot_general(
        a, b, (((0,), (0,)), ((), ())), preferred_element_type=jnp.float32
    )


def eliminate(m, pscr, qscr, count, pad, size):
    panel = PANEL
    lane = lax.broadcasted_iota(jnp.int32, (pad, size), 1)
    for block in reversed(range(size // panel)):
        base = block * panel
        rows = [m[pl.ds(base + r, pad, stride=size), :] for r in range(panel)]
        for k in reversed(range(panel)):
            col = base + k
            here = lane == col
            inv = 1.0 / rows[k][:, col : col + 1]
            pivot_row = jnp.where(here, 1.0, rows[k])
            scaled = pivot_row * inv
            for i in range(k):
                f = rows[i][:, col : col + 1]
                rows[i] = jnp.where(here, 0.0, rows[i]) - f * scaled
            if block:
                pscr[pl.ds(k * pad, pad), :] = jnp.where(
                    (lane >= base) & (lane < col), 0.0, pivot_row
                )
                qscr[pl.ds(k * pad, pad), :] = scaled
            m[pl.ds(col, pad, stride=size), :] = jnp.where(
                lane >= col, pivot_row * jnp.sqrt(inv), 0.0
            )
        if block:
            lane_m = lax.broadcasted_iota(jnp.int32, (base, size), 1)
            inside = (lane_m >= base) & (lane_m < base + panel)
            for n in range(count):
                ph, pm, plow = split3(pscr[pl.ds(n, panel, stride=pad), :])
                qh, qm, ql = split3(qscr[pl.ds(n, panel, stride=pad), :])
                right = jnp.concatenate([ph, pm, ph, plow, ph, pm], axis=0)
                left = jnp.concatenate([qh, qh, qm, qh, ql, qm], axis=0)
                update = tdot(left, right)[:base]
                spot = pl.ds(n * size, base)
                m[spot, :] = jnp.where(inside, 0.0, m[spot, :]) - update


def inverse_kernel(d_ref, e_ref, m, pscr, qscr):
    count, size, _ = d_ref.shape
    pad = m.shape[0] // size
    for n in range(count):
        m[pl.ds(n * size, size), :] = d_ref[n]
    for n in range(count, pad):
        m[pl.ds(n * size, size), :] = d_ref[0]
    eliminate(m, pscr, qscr, count, pad, size)
    for n in range(count):
        h, mid, low = split3(m[pl.ds(n * size, size), :])
        e = tdot(jnp.concatenate([h, h, mid], axis=0), jnp.concatenate([h, mid, h], axis=0))
        e_ref[n] = e.astype(e_ref.dtype)


def factor_kernel(d_ref, k_ref, m, pscr, qscr):
    count, size, _ = d_ref.shape
    pad = m.shape[0] // size
    for n in range(count):
        m[pl.ds(n * size, size), :] = d_ref[n]
    for n in range(count, pad):
        m[pl.ds(n * size, size), :] = d_ref[0]
    eliminate(m, pscr, qscr, count, pad, size)
    for n in range(count):
        k_ref[n] = m[pl.ds(n * size, size), :]


def run_factor(kernel, blocks, dtype):
    count, size, _ = blocks.shape
    pad = -(-count // 8) * 8
    return pl.pallas_call(
        kernel,
        out_shape=jax.ShapeDtypeStruct(blocks.shape, dtype),
        in_specs=[pl.BlockSpec(memory_space=pltpu.VMEM)],
        out_specs=pl.BlockSpec(memory_space=pltpu.VMEM),
        scratch_shapes=[
            pltpu.VMEM((pad * size, size), jnp.float32),
            pltpu.VMEM((PANEL * pad, size), jnp.float32),
            pltpu.VMEM((PANEL * pad, size), jnp.float32),
        ],
    )(blocks)


def build_diag(noise_block, shift_block, factor):
    noise_block = noise_block.astype(jnp.float32) * factor
    symmetric = (noise_block + jnp.swapaxes(noise_block, -1, -2)) * 0.5
    eye_block = jnp.eye(noise_block.shape[-1], dtype=jnp.float32)
    return symmetric + shift_block.astype(jnp.float32)[..., :, None] * eye_block


def row_factors(diag_own, coupling, inverse_near):
    product = jnp.einsum("rmab,rmbc->rmac", coupling, inverse_near, precision=highest)
    schur_block = diag_own - jnp.einsum("rmab,rmcb->rac", product, coupling, precision=highest)
    factor_diag = run_factor(factor_kernel, schur_block, jnp.float32)
    factor_off = -jnp.einsum("rab,rmbc->rmac", factor_diag, product, precision=highest)
    return (factor_diag, factor_off)


def body(diag_noise, couplings, shifts, near_devices, near_slots, vectors):
    dev_count = lax.axis_size("rows")
    my_index = lax.axis_index("rows")
    row_count = diag_noise.shape[0]
    block_size = diag_noise.shape[1]
    vec_count = vectors.shape[0]
    capacity = 3 * row_count // (dev_count - 1) + 2
    slot_total = dev_count * capacity
    request_count = 3 * row_count
    factor = 0.5 / math.sqrt(block_size)
    coupling_factor = 0.4 / math.sqrt(block_size)
    target = ((my_index - 1 - near_devices) % dev_count).reshape(-1)
    device_onehot = (target[:, None] == jnp.arange(dev_count, dtype=jnp.int32)[None, :]).astype(
        jnp.int32
    )
    running = jnp.cumsum(device_onehot, axis=0) - 1
    rank_within = jnp.sum(running * device_onehot, axis=1)
    position = target * capacity + rank_within
    source_index = (
        jnp.full((slot_total,), request_count, jnp.int32)
        .at[position]
        .set(jnp.arange(request_count, dtype=jnp.int32))
    )
    filled = source_index < request_count
    safe_source = jnp.minimum(source_index, request_count - 1)
    asked_slots = jnp.where(filled, near_slots.reshape(-1)[safe_source], -1)
    incoming = lax.all_to_all(
        asked_slots.reshape(dev_count, capacity), "rows", split_axis=0, concat_axis=0, tiled=True
    ).reshape(-1)
    served = jnp.maximum(incoming, 0)
    landing = (incoming[:, None] == jnp.arange(row_count, dtype=jnp.int32)[None, :]).astype(
        jnp.float32
    )
    diag_own = build_diag(diag_noise, shifts, factor)
    inverse_own = run_factor(inverse_kernel, diag_own, jnp.bfloat16)
    answer = inverse_own[served].reshape(dev_count, capacity, block_size, block_size)
    returned = lax.all_to_all(answer, "rows", split_axis=0, concat_axis=0, tiled=True)
    inverse_near = returned.reshape(slot_total, block_size, block_size)[position]
    inverse_near = inverse_near.reshape(row_count, 3, block_size, block_size).astype(jnp.float32)
    coupling = couplings.astype(jnp.float32) * coupling_factor
    factor_diag, factor_off = row_factors(diag_own, coupling, inverse_near)
    vector_rows = vectors.reshape(vec_count, row_count, block_size).transpose(1, 0, 2)
    left_product = jnp.einsum("rva,rab->rvb", vector_rows, factor_diag, precision=highest)
    outgoing = jnp.einsum("rva,rmab->rmvb", vector_rows, factor_off, precision=highest).reshape(
        request_count, vec_count, block_size
    )
    outgoing_slots = jnp.where(filled[:, None, None], outgoing[safe_source], 0.0).reshape(
        dev_count, capacity, vec_count, block_size
    )
    arrived = (
        lax.all_to_all(
            outgoing_slots.astype(jnp.bfloat16), "rows", split_axis=0, concat_axis=0, tiled=True
        )
        .astype(outgoing_slots.dtype)
        .reshape(slot_total, vec_count, block_size)
    )
    left_product = left_product + jnp.einsum("pr,pvb->rvb", landing, arrived, precision=highest)
    left_answer = left_product[served].reshape(dev_count, capacity, vec_count, block_size)
    pushed = jnp.einsum("rva,rmab->rmvb", left_product, coupling, precision=highest).reshape(
        request_count, vec_count, block_size
    )
    pushed_slots = jnp.where(filled[:, None, None], pushed[safe_source], 0.0).reshape(
        dev_count, capacity, vec_count, block_size
    )
    left_returned, pushed_arrived = (
        lax.all_to_all(left_answer.astype(jnp.bfloat16), "rows", split_axis=0, concat_axis=0, tiled=True),
        lax.all_to_all(pushed_slots.astype(jnp.bfloat16), "rows", split_axis=0, concat_axis=0, tiled=True),
    )
    left_near = left_returned.astype(jnp.float32).reshape(slot_total, vec_count, block_size)[position].reshape(
        row_count, 3, vec_count, block_size
    )
    middle_product = jnp.einsum("rva,rab->rvb", left_product, diag_own, precision=highest)
    middle_product = middle_product + jnp.einsum(
        "rmvb,rmab->rva", left_near, coupling, precision=highest
    )
    middle_product = middle_product + jnp.einsum(
        "pr,pvb->rvb",
        landing,
        pushed_arrived.astype(jnp.float32).reshape(slot_total, vec_count, block_size),
        precision=highest,
    )
    middle_answer = middle_product[served].reshape(dev_count, capacity, vec_count, block_size)
    middle_returned = lax.all_to_all(
        middle_answer.astype(jnp.bfloat16), "rows", split_axis=0, concat_axis=0, tiled=True
    ).astype(middle_answer.dtype)
    middle_near = middle_returned.reshape(slot_total, vec_count, block_size)[position].reshape(
        row_count, 3, vec_count, block_size
    )
    result = jnp.einsum("rvb,rab->rva", middle_product, factor_diag, precision=highest)
    result = result + jnp.einsum("rmvb,rmab->rva", middle_near, factor_off, precision=highest)
    return result.transpose(1, 0, 2).reshape(vec_count, row_count * block_size)


def solution(mesh):
    return jax.shard_map(
        body,
        mesh=mesh,
        in_specs=(
            P("rows", None, None),
            P("rows", None, None, None),
            P("rows", None),
            P("rows", None),
            P("rows", None),
            P(None, "rows"),
        ),
        out_specs=P(None, "rows"),
        check_vma=False,
    )
```

```python
import functools
import math

import jax
import jax.numpy as jnp
from jax import lax
from jax.experimental import pallas as pl
from jax.experimental.pallas import tpu as pltpu
from jax.sharding import PartitionSpec as P

highest = lax.Precision.HIGHEST
PANEL = 16


def split3(x):
    high = x.astype(jnp.bfloat16)
    rest = x - high.astype(jnp.float32)
    mid = rest.astype(jnp.bfloat16)
    low = (rest - mid.astype(jnp.float32)).astype(jnp.bfloat16)
    return high, mid, low


def tdot(a, b):
    return lax.dot_general(
        a, b, (((0,), (0,)), ((), ())), preferred_element_type=jnp.float32
    )


def eliminate(m, pscr, qscr, count, pad, size):
    panel = PANEL
    lane = lax.broadcasted_iota(jnp.int32, (pad, size), 1)
    for block in reversed(range(size // panel)):
        base = block * panel
        rows = [m[pl.ds(base + r, pad, stride=size), :] for r in range(panel)]
        for k in reversed(range(panel)):
            col = base + k
            here = lane == col
            inv = 1.0 / rows[k][:, col : col + 1]
            pivot_row = jnp.where(here, 1.0, rows[k])
            scaled = pivot_row * inv
            for i in range(k):
                f = rows[i][:, col : col + 1]
                rows[i] = jnp.where(here, 0.0, rows[i]) - f * scaled
            if block:
                pscr[pl.ds(k * pad, pad), :] = jnp.where(
                    (lane >= base) & (lane < col), 0.0, pivot_row
                )
                qscr[pl.ds(k * pad, pad), :] = scaled
            m[pl.ds(col, pad, stride=size), :] = jnp.where(
                lane >= col, pivot_row * jnp.sqrt(inv), 0.0
            )
        if block:
            lane_m = lax.broadcasted_iota(jnp.int32, (base, size), 1)
            inside = (lane_m >= base) & (lane_m < base + panel)
            for n in range(count):
                ph, pm, plow = split3(pscr[pl.ds(n, panel, stride=pad), :])
                qh, qm, ql = split3(qscr[pl.ds(n, panel, stride=pad), :])
                right = jnp.concatenate([ph, pm, ph, plow, ph, pm], axis=0)
                left = jnp.concatenate([qh, qh, qm, qh, ql, qm], axis=0)
                update = tdot(left, right)[:base]
                spot = pl.ds(n * size, base)
                m[spot, :] = jnp.where(inside, 0.0, m[spot, :]) - update


def joined(*parts):
    return jnp.concatenate(parts, axis=-1)


def split2(x):
    high = x.astype(jnp.bfloat16)
    return high, (x - high.astype(jnp.float32)).astype(jnp.bfloat16)


def dot_nn(a, b):
    return jnp.dot(a, b, preferred_element_type=jnp.float32)


def dot_nt(a, b):
    return lax.dot_general(
        a, b, (((1,), (1,)), ((), ())), preferred_element_type=jnp.float32
    )


def inverse_kernel(d_ref, e_ref, g_ref, m, pscr, qscr):
    count, size, _ = d_ref.shape
    half = size // 2
    pad = m.shape[0] // size
    for n in range(count):
        m[pl.ds(n * size, size), :] = d_ref[n]
    for n in range(count, pad):
        m[pl.ds(n * size, size), :] = d_ref[0]
    eliminate(m, pscr, qscr, count, pad, size)
    row = lax.broadcasted_iota(jnp.int32, (half, half), 0)
    col = lax.broadcasted_iota(jnp.int32, (half, half), 1)
    row_full = lax.broadcasted_iota(jnp.int32, (size, size), 0)
    col_full = lax.broadcasted_iota(jnp.int32, (size, size), 1)
    for n in range(count):
        h, mid, low = split3(m[pl.ds(n * size, size), :])
        e = tdot(jnp.concatenate([h, h, mid], axis=0), jnp.concatenate([h, mid, h], axis=0))
        left = jnp.where(row >= col, e[:half, :half], e[half:, half:])
        e_ref[n] = joined(left, e[:half, half:]).astype(e_ref.dtype)
        diag = jnp.sum(jnp.where(row_full == col_full, e, 0.0), axis=0, keepdims=True)
        g_ref[n] = jnp.broadcast_to(diag, g_ref.shape[1:]).astype(g_ref.dtype)


def answer_kernel(capacity, served_ref, e_ref, g_ref, out_ref):
    half, size = e_ref.shape[1:]
    tail = g_ref.shape[1]
    row = lax.broadcasted_iota(jnp.int32, (tail, size), 0)

    def step(t, carry):
        tile = jnp.zeros((tail, size), jnp.float32)
        for c in range(capacity):
            source = served_ref[t * capacity + c]
            out_ref[t, pl.ds(c * half, half), :] = e_ref[source]
            tile = jnp.where(row == c, g_ref[source].astype(jnp.float32), tile)
        out_ref[t, pl.ds(capacity * half, tail), :] = tile.astype(out_ref.dtype)
        return carry

    lax.fori_loop(0, out_ref.shape[0], step, 0)


def factor_kernel(
    capacity, scale, target_ref, rank_ref, near_ref, c_ref, d_ref, v_ref,
    k_ref, fh_ref, fl_ref, left_ref, out_ref, m, pscr, qscr,
):
    count, size, _ = d_ref.shape
    half = size // 2
    pad = m.shape[0] // size
    tail = near_ref.shape[1] - capacity * half
    row = lax.broadcasted_iota(jnp.int32, (half, half), 0)
    col = lax.broadcasted_iota(jnp.int32, (half, half), 1)
    tail_row = lax.broadcasted_iota(jnp.int32, (tail, size), 0)

    def schur(n, carry):
        total = d_ref[n]
        for k in range(3):
            t = target_ref[3 * n + k]
            c = rank_ref[3 * n + k]
            packed = near_ref[t, pl.ds(pl.multiple_of(c * half, half), half), :]
            packed = packed.astype(jnp.float32)
            tile = near_ref[t, pl.ds(capacity * half, tail), :].astype(jnp.float32)
            diag = jnp.sum(jnp.where(tail_row == c, tile, 0.0), axis=0, keepdims=True)
            flipped = packed.T
            part = packed[:, :half]
            part_t = flipped[:half, :]
            first = jnp.where(row >= col, part, part_t)
            last = jnp.where(row < col, part, part_t)
            last = jnp.where(row == col, diag[:, half:], last)
            inverse = jnp.concatenate(
                [joined(first, packed[:, half:]), joined(flipped[half:, :], last)], axis=0
            ).astype(jnp.bfloat16)
            coupling = c_ref[n, k]
            f = dot_nn(coupling, inverse) * scale
            high, low = split2(f)
            fh_ref[n, k] = high
            fl_ref[n, k] = low
            total = total - scale * dot_nt(joined(high, low), joined(coupling, coupling))
        m[pl.ds(pl.multiple_of(n * size, size), size), :] = total
        return carry

    lax.fori_loop(0, count, schur, 0, unroll=2)
    for n in range(count, pad):
        m[pl.ds(n * size, size), :] = d_ref[0]
    eliminate(m, pscr, qscr, count, pad, size)
    out_ref[...] = jnp.zeros_like(out_ref)
    for n in range(count):
        k = m[pl.ds(n * size, size), :]
        k_ref[n] = k
        kh, kl = split2(k)
        vh, vl = split2(v_ref[:, n * size : (n + 1) * size])
        left = dot_nn(joined(vh, vh, vl), jnp.concatenate([kh, kl, kh], axis=0))
        left_ref[n] = left
        lh, ll = split2(left)
        for k in range(3):
            r = 3 * n + k
            fh, fl = fh_ref[n, k], fl_ref[n, k]
            sent = dot_nn(joined(lh, lh, ll), jnp.concatenate([fh, fl, fh], axis=0))
            out_ref[target_ref[r] * capacity + rank_ref[r]] = (-sent).astype(out_ref.dtype)


def add_arrived(total, incoming_ref, get, slots):
    count = total.shape[0] - 1
    for s in range(slots):
        wanted = incoming_ref[s]
        spot = jnp.where(wanted < 0, count, wanted)
        total[spot] = total[spot] + get(s).astype(jnp.float32)


def left_kernel(
    capacity, scale, target_ref, rank_ref, incoming_ref, arrived_ref, left_in, c_ref,
    left_ref, out_ref, total,
):
    count = left_in.shape[0]
    slots = arrived_ref.shape[0]
    total[:count] = left_in[...]
    total[count] = jnp.zeros_like(total[count])
    add_arrived(total, incoming_ref, lambda s: arrived_ref[s], slots)
    left_ref[...] = total[:count]
    for s in range(slots):
        spot = s // capacity * 2 * capacity + s % capacity
        out_ref[spot] = total[jnp.maximum(incoming_ref[s], 0)].astype(out_ref.dtype)
        out_ref[spot + capacity] = jnp.zeros_like(out_ref[spot + capacity])
    for n in range(count):
        lh, ll = split2(total[n])
        both = joined(lh, ll)
        for k in range(3):
            r = 3 * n + k
            coupling = c_ref[n, k]
            sent = scale * dot_nn(both, jnp.concatenate([coupling, coupling], axis=0))
            spot = target_ref[r] * (2 * capacity) + capacity + rank_ref[r]
            out_ref[spot] = sent.astype(out_ref.dtype)


def middle_kernel(
    capacity, scale, target_ref, rank_ref, incoming_ref, arrived_ref, own_ref, c_ref,
    middle_ref, out_ref, total,
):
    count = own_ref.shape[0]
    slots = out_ref.shape[0]
    total[count] = jnp.zeros_like(total[count])
    for n in range(count):
        near = own_ref[n]
        for k in range(3):
            r = 3 * n + k
            got = arrived_ref[target_ref[r] * (2 * capacity) + rank_ref[r]]
            near = near + scale * dot_nt(got, c_ref[n, k])
        total[n] = near
    add_arrived(
        total,
        incoming_ref,
        lambda s: arrived_ref[s // capacity * 2 * capacity + capacity + s % capacity],
        slots,
    )
    middle_ref[...] = total[:count]
    for s in range(slots):
        out_ref[s] = total[jnp.maximum(incoming_ref[s], 0)].astype(out_ref.dtype)


def final_kernel(
    capacity, target_ref, rank_ref, arrived_ref, middle_ref, k_ref, fh_ref, fl_ref, out_ref
):
    count, size, _ = k_ref.shape
    for n in range(count):
        part = middle_ref[n]
        for k in range(3):
            r = 3 * n + k
            got = arrived_ref[target_ref[r] * capacity + rank_ref[r]]
            part = part - dot_nt(joined(got, got), joined(fh_ref[n, k], fl_ref[n, k]))
        ph, plow = split2(part)
        kh, kl = split2(k_ref[n])
        out_ref[:, n * size : (n + 1) * size] = dot_nt(
            joined(ph, ph, plow), joined(kh, kl, kh)
        )


def call(kernel, scalars, arrays, shapes, scratch=()):
    smem = pl.BlockSpec(memory_space=pltpu.SMEM)
    vmem = pl.BlockSpec(memory_space=pltpu.VMEM)
    return pl.pallas_call(
        kernel,
        out_shape=[jax.ShapeDtypeStruct(shape, dtype) for shape, dtype in shapes],
        in_specs=[smem] * len(scalars) + [vmem] * len(arrays),
        out_specs=[vmem] * len(shapes),
        scratch_shapes=[pltpu.VMEM(shape, jnp.float32) for shape in scratch],
    )(*scalars, *arrays)


def build_diag(noise_block, shift_block, factor):
    noise_block = noise_block.astype(jnp.float32) * factor
    symmetric = (noise_block + jnp.swapaxes(noise_block, -1, -2)) * 0.5
    eye_block = jnp.eye(noise_block.shape[-1], dtype=jnp.float32)
    return symmetric + shift_block.astype(jnp.float32)[..., :, None] * eye_block


def exchange(x, dev_count):
    shape = x.shape
    x = x.reshape(dev_count, -1, *shape[1:])
    x = lax.all_to_all(x, "rows", split_axis=0, concat_axis=0, tiled=True)
    return x.reshape(shape)


def body(diag_noise, couplings, shifts, near_devices, near_slots, vectors):
    dev_count = lax.axis_size("rows")
    my_index = lax.axis_index("rows")
    row_count = diag_noise.shape[0]
    block_size = diag_noise.shape[1]
    vec_count = vectors.shape[0]
    capacity = 3 * row_count // (dev_count - 1) + 2
    slot_total = dev_count * capacity
    factor = 0.5 / math.sqrt(block_size)
    coupling_factor = 0.4 / math.sqrt(block_size)
    target = ((my_index - 1 - near_devices) % dev_count).reshape(-1)
    device_onehot = (target[:, None] == jnp.arange(dev_count, dtype=jnp.int32)[None, :]).astype(
        jnp.int32
    )
    running = jnp.cumsum(device_onehot, axis=0) - 1
    rank = jnp.sum(running * device_onehot, axis=1)
    position = target * capacity + rank
    hit = position[None, :] == jnp.arange(slot_total, dtype=jnp.int32)[:, None]
    asked_slots = jnp.sum(jnp.where(hit, near_slots.reshape(1, -1) + 1, 0), axis=1) - 1
    incoming = exchange(asked_slots, dev_count)
    served = jnp.maximum(incoming, 0)
    diag_own = build_diag(diag_noise, shifts, factor)

    bf16, f32 = jnp.bfloat16, jnp.float32
    half = block_size // 2
    tail = 16
    pad = -(-row_count // 8) * 8
    work = ((pad * block_size, block_size),) + ((PANEL * pad, block_size),) * 2
    packed, diags = call(
        inverse_kernel,
        (),
        (diag_own,),
        (((row_count, half, block_size), bf16), ((row_count, tail, block_size), bf16)),
        work,
    )
    (answer,) = call(
        functools.partial(answer_kernel, capacity),
        (served,),
        (packed, diags),
        (((dev_count, capacity * half + tail, block_size), bf16),),
    )
    near = exchange(answer, dev_count)
    rows_shape = (row_count, vec_count, block_size)
    total_shape = ((row_count + 1, vec_count, block_size),)
    slots_shape = (slot_total, vec_count, block_size)
    f_shape = (row_count, 3, block_size, block_size)
    k_all, f_high, f_low, left, outgoing = call(
        functools.partial(factor_kernel, capacity, coupling_factor),
        (target, rank),
        (near, couplings, diag_own, vectors),
        (
            ((row_count, block_size, block_size), f32),
            (f_shape, bf16),
            (f_shape, bf16),
            (rows_shape, f32),
            (slots_shape, bf16),
        ),
        work,
    )
    arrived = exchange(outgoing, dev_count)
    left, outgoing = call(
        functools.partial(left_kernel, capacity, coupling_factor),
        (target, rank, incoming),
        (arrived, left, couplings),
        ((rows_shape, f32), ((2 * slot_total, vec_count, block_size), bf16)),
        total_shape,
    )
    arrived = exchange(outgoing, dev_count)
    own = jnp.einsum("rva,rab->rvb", left, diag_own, precision=highest)
    middle, outgoing = call(
        functools.partial(middle_kernel, capacity, coupling_factor),
        (target, rank, incoming),
        (arrived, own, couplings),
        ((rows_shape, f32), (slots_shape, bf16)),
        total_shape,
    )
    arrived = exchange(outgoing, dev_count)
    (result,) = call(
        functools.partial(final_kernel, capacity),
        (target, rank),
        (arrived, middle, k_all, f_high, f_low),
        ((vectors.shape, f32),),
    )
    return result


def solution(mesh):
    return jax.shard_map(
        body,
        mesh=mesh,
        in_specs=(
            P("rows", None, None),
            P("rows", None, None, None),
            P("rows", None),
            P("rows", None),
            P("rows", None),
            P(None, "rows"),
        ),
        out_specs=P(None, "rows"),
        check_vma=False,
    )
```

```python
import functools
import math

import jax
import jax.numpy as jnp
from jax import lax
from jax.experimental import pallas as pl
from jax.experimental.pallas import tpu as pltpu
from jax.sharding import PartitionSpec as P

highest = lax.Precision.HIGHEST
PANEL = 16
GROUP = 4


def split3(x):
    high = x.astype(jnp.bfloat16)
    rest = x - high.astype(jnp.float32)
    mid = rest.astype(jnp.bfloat16)
    low = (rest - mid.astype(jnp.float32)).astype(jnp.bfloat16)
    return high, mid, low


def tdot(a, b):
    return lax.dot_general(
        a, b, (((0,), (0,)), ((), ())), preferred_element_type=jnp.float32
    )


def eliminate(m, pscr, qscr, count, pad, size):
    panel = PANEL
    lane = lax.broadcasted_iota(jnp.int32, (pad, size), 1)
    for block in reversed(range(size // panel)):
        base = block * panel
        rows = [m[pl.ds(base + r, pad, stride=size), :] for r in range(panel)]
        for k in reversed(range(panel)):
            col = base + k
            here = lane == col
            if (k + 1) % GROUP == 0:
                first = k + 1 - GROUP
                tile = {
                    (i, c): jnp.broadcast_to(rows[i][:, base + c : base + c + 1], (pad, size))
                    for c in range(first, k + 1)
                    for i in range(c + 1)
                }
            inv = 1.0 / tile[k, k]
            for c in reversed(range(first, k)):
                ratio = tile[c, k] * inv
                for i in range(c + 1):
                    tile[i, c] = tile[i, c] - tile[i, k] * ratio
            pivot_row = jnp.where(here, 1.0, rows[k])
            scaled = pivot_row * inv
            for i in range(k):
                rows[i] = jnp.where(here, 0.0, rows[i]) - tile[i, k] * scaled
            if block:
                pscr[pl.ds(k * pad, pad), :] = jnp.where(
                    (lane >= base) & (lane < col), 0.0, pivot_row
                )
                qscr[pl.ds(k * pad, pad), :] = scaled
            m[pl.ds(col, pad, stride=size), :] = jnp.where(
                lane >= col, pivot_row * jnp.sqrt(inv), 0.0
            )
        if block:
            lane_m = lax.broadcasted_iota(jnp.int32, (base, size), 1)
            inside = (lane_m >= base) & (lane_m < base + panel)
            for n in range(count):
                ph, pm, plow = split3(pscr[pl.ds(n, panel, stride=pad), :])
                qh, qm, ql = split3(qscr[pl.ds(n, panel, stride=pad), :])
                right = jnp.concatenate([ph, pm, ph, plow, ph, pm], axis=0)
                left = jnp.concatenate([qh, qh, qm, qh, ql, qm], axis=0)
                update = tdot(left, right)[:base]
                spot = pl.ds(n * size, base)
                m[spot, :] = jnp.where(inside, 0.0, m[spot, :]) - update


def joined(*parts):
    return jnp.concatenate(parts, axis=-1)


def split2(x):
    high = x.astype(jnp.bfloat16)
    return high, (x - high.astype(jnp.float32)).astype(jnp.bfloat16)


def dot_nn(a, b):
    return jnp.dot(a, b, preferred_element_type=jnp.float32)


def dot_nt(a, b):
    return lax.dot_general(
        a, b, (((1,), (1,)), ((), ())), preferred_element_type=jnp.float32
    )


def inverse_kernel(d_ref, e_ref, g_ref, m, pscr, qscr):
    count, size, _ = d_ref.shape
    half = size // 2
    pad = m.shape[0] // size
    for n in range(count):
        m[pl.ds(n * size, size), :] = d_ref[n]
    for n in range(count, pad):
        m[pl.ds(n * size, size), :] = d_ref[0]
    eliminate(m, pscr, qscr, count, pad, size)
    row = lax.broadcasted_iota(jnp.int32, (half, half), 0)
    col = lax.broadcasted_iota(jnp.int32, (half, half), 1)
    row_full = lax.broadcasted_iota(jnp.int32, (size, size), 0)
    col_full = lax.broadcasted_iota(jnp.int32, (size, size), 1)
    for n in range(count):
        h, mid, low = split3(m[pl.ds(n * size, size), :])
        e = tdot(jnp.concatenate([h, h, mid], axis=0), jnp.concatenate([h, mid, h], axis=0))
        left = jnp.where(row >= col, e[:half, :half], e[half:, half:])
        e_ref[n] = joined(left, e[:half, half:]).astype(e_ref.dtype)
        diag = jnp.sum(jnp.where(row_full == col_full, e, 0.0), axis=0, keepdims=True)
        g_ref[n] = jnp.broadcast_to(diag, g_ref.shape[1:]).astype(g_ref.dtype)


def answer_kernel(capacity, served_ref, e_ref, g_ref, out_ref):
    half, size = e_ref.shape[1:]
    tail = g_ref.shape[1]
    row = lax.broadcasted_iota(jnp.int32, (tail, size), 0)

    def step(t, carry):
        tile = jnp.zeros((tail, size), jnp.float32)
        for c in range(capacity):
            source = served_ref[t * capacity + c]
            out_ref[t, pl.ds(c * half, half), :] = e_ref[source]
            tile = jnp.where(row == c, g_ref[source].astype(jnp.float32), tile)
        out_ref[t, pl.ds(capacity * half, tail), :] = tile.astype(out_ref.dtype)
        return carry

    lax.fori_loop(0, out_ref.shape[0], step, 0)


def factor_kernel(
    capacity, scale, target_ref, rank_ref, near_ref, c_ref, d_ref, v_ref,
    k_ref, fh_ref, fl_ref, left_ref, out_ref, m, pscr, qscr,
):
    count, size, _ = d_ref.shape
    half = size // 2
    pad = m.shape[0] // size
    tail = near_ref.shape[1] - capacity * half
    row = lax.broadcasted_iota(jnp.int32, (half, half), 0)
    col = lax.broadcasted_iota(jnp.int32, (half, half), 1)
    tail_row = lax.broadcasted_iota(jnp.int32, (tail, size), 0)

    def schur(n, carry):
        total = d_ref[n]
        for k in range(3):
            t = target_ref[3 * n + k]
            c = rank_ref[3 * n + k]
            packed = near_ref[t, pl.ds(pl.multiple_of(c * half, half), half), :]
            packed = packed.astype(jnp.float32)
            tile = near_ref[t, pl.ds(capacity * half, tail), :].astype(jnp.float32)
            diag = jnp.sum(jnp.where(tail_row == c, tile, 0.0), axis=0, keepdims=True)
            flipped = packed.T
            part = packed[:, :half]
            part_t = flipped[:half, :]
            first = jnp.where(row >= col, part, part_t)
            last = jnp.where(row < col, part, part_t)
            last = jnp.where(row == col, diag[:, half:], last)
            inverse = jnp.concatenate(
                [joined(first, packed[:, half:]), joined(flipped[half:, :], last)], axis=0
            ).astype(jnp.bfloat16)
            coupling = c_ref[n, k]
            f = dot_nn(coupling, inverse) * scale
            high, low = split2(f)
            fh_ref[n, k] = high
            fl_ref[n, k] = low
            total = total - scale * dot_nt(joined(high, low), joined(coupling, coupling))
        m[pl.ds(pl.multiple_of(n * size, size), size), :] = total
        return carry

    lax.fori_loop(0, count, schur, 0, unroll=2)
    for n in range(count, pad):
        m[pl.ds(n * size, size), :] = d_ref[0]
    eliminate(m, pscr, qscr, count, pad, size)
    out_ref[...] = jnp.zeros_like(out_ref)
    for n in range(count):
        k = m[pl.ds(n * size, size), :]
        k_ref[n] = k
        kh, kl = split2(k)
        vh, vl = split2(v_ref[:, n * size : (n + 1) * size])
        left = dot_nn(joined(vh, vh, vl), jnp.concatenate([kh, kl, kh], axis=0))
        left_ref[n] = left
        lh, ll = split2(left)
        for k in range(3):
            r = 3 * n + k
            fh, fl = fh_ref[n, k], fl_ref[n, k]
            sent = dot_nn(joined(lh, lh, ll), jnp.concatenate([fh, fl, fh], axis=0))
            out_ref[target_ref[r] * capacity + rank_ref[r]] = (-sent).astype(out_ref.dtype)


def add_arrived(total, incoming_ref, get, slots):
    count = total.shape[0] - 1
    for s in range(slots):
        wanted = incoming_ref[s]
        spot = jnp.where(wanted < 0, count, wanted)
        total[spot] = total[spot] + get(s).astype(jnp.float32)


def left_kernel(
    capacity, scale, target_ref, rank_ref, incoming_ref, arrived_ref, left_in, c_ref,
    left_ref, out_ref, total,
):
    count = left_in.shape[0]
    slots = arrived_ref.shape[0]
    total[:count] = left_in[...]
    total[count] = jnp.zeros_like(total[count])
    add_arrived(total, incoming_ref, lambda s: arrived_ref[s], slots)
    left_ref[...] = total[:count]
    for s in range(slots):
        spot = s // capacity * 2 * capacity + s % capacity
        out_ref[spot] = total[jnp.maximum(incoming_ref[s], 0)].astype(out_ref.dtype)
        out_ref[spot + capacity] = jnp.zeros_like(out_ref[spot + capacity])
    for n in range(count):
        lh, ll = split2(total[n])
        both = joined(lh, ll)
        for k in range(3):
            r = 3 * n + k
            coupling = c_ref[n, k]
            sent = scale * dot_nn(both, jnp.concatenate([coupling, coupling], axis=0))
            spot = target_ref[r] * (2 * capacity) + capacity + rank_ref[r]
            out_ref[spot] = sent.astype(out_ref.dtype)


def middle_kernel(
    capacity, scale, target_ref, rank_ref, incoming_ref, arrived_ref, own_ref, c_ref,
    middle_ref, out_ref, total,
):
    count = own_ref.shape[0]
    slots = out_ref.shape[0]
    total[count] = jnp.zeros_like(total[count])
    for n in range(count):
        near = own_ref[n]
        for k in range(3):
            r = 3 * n + k
            got = arrived_ref[target_ref[r] * (2 * capacity) + rank_ref[r]]
            near = near + scale * dot_nt(got, c_ref[n, k])
        total[n] = near
    add_arrived(
        total,
        incoming_ref,
        lambda s: arrived_ref[s // capacity * 2 * capacity + capacity + s % capacity],
        slots,
    )
    middle_ref[...] = total[:count]
    for s in range(slots):
        out_ref[s] = total[jnp.maximum(incoming_ref[s], 0)].astype(out_ref.dtype)


def final_kernel(
    capacity, target_ref, rank_ref, arrived_ref, middle_ref, k_ref, fh_ref, fl_ref, out_ref
):
    count, size, _ = k_ref.shape
    for n in range(count):
        part = middle_ref[n]
        for k in range(3):
            r = 3 * n + k
            got = arrived_ref[target_ref[r] * capacity + rank_ref[r]]
            part = part - dot_nt(joined(got, got), joined(fh_ref[n, k], fl_ref[n, k]))
        ph, plow = split2(part)
        kh, kl = split2(k_ref[n])
        out_ref[:, n * size : (n + 1) * size] = dot_nt(
            joined(ph, ph, plow), joined(kh, kl, kh)
        )


def call(kernel, scalars, arrays, shapes, scratch=()):
    smem = pl.BlockSpec(memory_space=pltpu.SMEM)
    vmem = pl.BlockSpec(memory_space=pltpu.VMEM)
    return pl.pallas_call(
        kernel,
        out_shape=[jax.ShapeDtypeStruct(shape, dtype) for shape, dtype in shapes],
        in_specs=[smem] * len(scalars) + [vmem] * len(arrays),
        out_specs=[vmem] * len(shapes),
        scratch_shapes=[pltpu.VMEM(shape, jnp.float32) for shape in scratch],
    )(*scalars, *arrays)


def build_diag(noise_block, shift_block, factor):
    noise_block = noise_block.astype(jnp.float32) * factor
    symmetric = (noise_block + jnp.swapaxes(noise_block, -1, -2)) * 0.5
    eye_block = jnp.eye(noise_block.shape[-1], dtype=jnp.float32)
    return symmetric + shift_block.astype(jnp.float32)[..., :, None] * eye_block


def exchange(x, dev_count):
    shape = x.shape
    x = x.reshape(dev_count, -1, *shape[1:])
    x = lax.all_to_all(x, "rows", split_axis=0, concat_axis=0, tiled=True)
    return x.reshape(shape)


def body(diag_noise, couplings, shifts, near_devices, near_slots, vectors):
    dev_count = lax.axis_size("rows")
    my_index = lax.axis_index("rows")
    row_count = diag_noise.shape[0]
    block_size = diag_noise.shape[1]
    vec_count = vectors.shape[0]
    capacity = 3 * row_count // (dev_count - 1) + 2
    slot_total = dev_count * capacity
    factor = 0.5 / math.sqrt(block_size)
    coupling_factor = 0.4 / math.sqrt(block_size)
    target = ((my_index - 1 - near_devices) % dev_count).reshape(-1)
    device_onehot = (target[:, None] == jnp.arange(dev_count, dtype=jnp.int32)[None, :]).astype(
        jnp.int32
    )
    running = jnp.cumsum(device_onehot, axis=0) - 1
    rank = jnp.sum(running * device_onehot, axis=1)
    position = target * capacity + rank
    hit = position[None, :] == jnp.arange(slot_total, dtype=jnp.int32)[:, None]
    asked_slots = jnp.sum(jnp.where(hit, near_slots.reshape(1, -1) + 1, 0), axis=1) - 1
    incoming = exchange(asked_slots, dev_count)
    served = jnp.maximum(incoming, 0)
    diag_own = build_diag(diag_noise, shifts, factor)

    bf16, f32 = jnp.bfloat16, jnp.float32
    half = block_size // 2
    tail = 16
    pad = -(-row_count // 8) * 8
    work = ((pad * block_size, block_size),) + ((PANEL * pad, block_size),) * 2
    packed, diags = call(
        inverse_kernel,
        (),
        (diag_own,),
        (((row_count, half, block_size), bf16), ((row_count, tail, block_size), bf16)),
        work,
    )
    (answer,) = call(
        functools.partial(answer_kernel, capacity),
        (served,),
        (packed, diags),
        (((dev_count, capacity * half + tail, block_size), bf16),),
    )
    near = exchange(answer, dev_count)
    rows_shape = (row_count, vec_count, block_size)
    total_shape = ((row_count + 1, vec_count, block_size),)
    slots_shape = (slot_total, vec_count, block_size)
    f_shape = (row_count, 3, block_size, block_size)
    k_all, f_high, f_low, left, outgoing = call(
        functools.partial(factor_kernel, capacity, coupling_factor),
        (target, rank),
        (near, couplings, diag_own, vectors),
        (
            ((row_count, block_size, block_size), f32),
            (f_shape, bf16),
            (f_shape, bf16),
            (rows_shape, f32),
            (slots_shape, bf16),
        ),
        work,
    )
    arrived = exchange(outgoing, dev_count)
    left, outgoing = call(
        functools.partial(left_kernel, capacity, coupling_factor),
        (target, rank, incoming),
        (arrived, left, couplings),
        ((rows_shape, f32), ((2 * slot_total, vec_count, block_size), bf16)),
        total_shape,
    )
    arrived = exchange(outgoing, dev_count)
    own = jnp.einsum("rva,rab->rvb", left, diag_own, precision=highest)
    middle, outgoing = call(
        functools.partial(middle_kernel, capacity, coupling_factor),
        (target, rank, incoming),
        (arrived, own, couplings),
        ((rows_shape, f32), (slots_shape, bf16)),
        total_shape,
    )
    arrived = exchange(outgoing, dev_count)
    (result,) = call(
        functools.partial(final_kernel, capacity),
        (target, rank),
        (arrived, middle, k_all, f_high, f_low),
        ((vectors.shape, f32),),
    )
    return result


def solution(mesh):
    return jax.shard_map(
        body,
        mesh=mesh,
        in_specs=(
            P("rows", None, None),
            P("rows", None, None, None),
            P("rows", None),
            P("rows", None),
            P("rows", None),
            P(None, "rows"),
        ),
        out_specs=P(None, "rows"),
        check_vma=False,
    )
```

```python
import functools
import math

import jax
import jax.numpy as jnp
from jax import lax
from jax.experimental import pallas as pl
from jax.experimental.pallas import tpu as pltpu
from jax.sharding import PartitionSpec as P

highest = lax.Precision.HIGHEST
PANEL = 16
GROUP = 4


def split3(x):
    high = x.astype(jnp.bfloat16)
    rest = x - high.astype(jnp.float32)
    mid = rest.astype(jnp.bfloat16)
    low = (rest - mid.astype(jnp.float32)).astype(jnp.bfloat16)
    return high, mid, low


def tdot(a, b):
    return lax.dot_general(
        a, b, (((0,), (0,)), ((), ())), preferred_element_type=jnp.float32
    )


def eliminate(m, pscr, qscr, count, pad, size):
    panel = PANEL
    lane = lax.broadcasted_iota(jnp.int32, (pad, size), 1)
    for block in reversed(range(size // panel)):
        base = block * panel
        rows = [m[pl.ds(base + r, pad, stride=size), :] for r in range(panel)]
        for k in reversed(range(panel)):
            col = base + k
            here = lane == col
            if (k + 1) % GROUP == 0:
                first = k + 1 - GROUP
                tile = {
                    (i, c): jnp.broadcast_to(rows[i][:, base + c : base + c + 1], (pad, size))
                    for c in range(first, k + 1)
                    for i in range(c + 1)
                }
            inv = 1.0 / tile[k, k]
            for c in reversed(range(first, k)):
                ratio = tile[c, k] * inv
                for i in range(c + 1):
                    tile[i, c] = tile[i, c] - tile[i, k] * ratio
            pivot_row = jnp.where(here, 1.0, rows[k])
            scaled = pivot_row * inv
            for i in range(k):
                rows[i] = jnp.where(here, 0.0, rows[i]) - tile[i, k] * scaled
            if block:
                pscr[pl.ds(k * pad, pad), :] = jnp.where(
                    (lane >= base) & (lane < col), 0.0, pivot_row
                )
                qscr[pl.ds(k * pad, pad), :] = scaled
            m[pl.ds(col, pad, stride=size), :] = jnp.where(
                lane >= col, pivot_row * jnp.sqrt(inv), 0.0
            )
        if block:
            lane_m = lax.broadcasted_iota(jnp.int32, (base, size), 1)
            inside = (lane_m >= base) & (lane_m < base + panel)
            for n in range(count):
                ph, pm, plow = split3(pscr[pl.ds(n, panel, stride=pad), :])
                qh, qm, ql = split3(qscr[pl.ds(n, panel, stride=pad), :])
                right = jnp.concatenate([ph, pm, ph, plow, ph, pm], axis=0)
                left = jnp.concatenate([qh, qh, qm, qh, ql, qm], axis=0)
                update = tdot(left, right)[:base]
                spot = pl.ds(n * size, base)
                m[spot, :] = jnp.where(inside, 0.0, m[spot, :]) - update


def joined(*parts):
    return jnp.concatenate(parts, axis=-1)


def split2(x):
    high = x.astype(jnp.bfloat16)
    return high, (x - high.astype(jnp.float32)).astype(jnp.bfloat16)


def dot_nn(a, b):
    return jnp.dot(a, b, preferred_element_type=jnp.float32)


def dot_nt(a, b):
    return lax.dot_general(
        a, b, (((1,), (1,)), ((), ())), preferred_element_type=jnp.float32
    )


def inverse_kernel(d_ref, e_ref, g_ref, m, pscr, qscr):
    count, size, _ = d_ref.shape
    half = size // 2
    pad = m.shape[0] // size
    for n in range(count):
        m[pl.ds(n * size, size), :] = d_ref[n]
    for n in range(count, pad):
        m[pl.ds(n * size, size), :] = d_ref[0]
    eliminate(m, pscr, qscr, count, pad, size)
    row = lax.broadcasted_iota(jnp.int32, (half, half), 0)
    col = lax.broadcasted_iota(jnp.int32, (half, half), 1)
    row_full = lax.broadcasted_iota(jnp.int32, (size, size), 0)
    col_full = lax.broadcasted_iota(jnp.int32, (size, size), 1)
    for n in range(count):
        h, mid, low = split3(m[pl.ds(n * size, size), :])
        e = tdot(jnp.concatenate([h, h, mid], axis=0), jnp.concatenate([h, mid, h], axis=0))
        left = jnp.where(row >= col, e[:half, :half], e[half:, half:])
        e_ref[n] = joined(left, e[:half, half:]).astype(e_ref.dtype)
        diag = jnp.sum(jnp.where(row_full == col_full, e, 0.0), axis=0, keepdims=True)
        g_ref[n] = jnp.broadcast_to(diag, g_ref.shape[1:]).astype(g_ref.dtype)


def answer_kernel(capacity, served_ref, e_ref, g_ref, out_ref):
    half, size = e_ref.shape[1:]
    tail = g_ref.shape[1]
    row = lax.broadcasted_iota(jnp.int32, (tail, size), 0)

    def step(t, carry):
        tile = jnp.zeros((tail, size), jnp.float32)
        for c in range(capacity):
            source = served_ref[t * capacity + c]
            out_ref[t, pl.ds(c * half, half), :] = e_ref[source]
            tile = jnp.where(row == c, g_ref[source].astype(jnp.float32), tile)
        out_ref[t, pl.ds(capacity * half, tail), :] = tile.astype(out_ref.dtype)
        return carry

    lax.fori_loop(0, out_ref.shape[0], step, 0, unroll=8)


def factor_kernel(
    capacity, scale, target_ref, rank_ref, near_ref, c_ref, d_ref, v_ref,
    k_ref, fh_ref, fl_ref, left_ref, out_ref, m, pscr, qscr,
):
    count, size, _ = d_ref.shape
    half = size // 2
    pad = m.shape[0] // size
    tail = near_ref.shape[1] - capacity * half
    row = lax.broadcasted_iota(jnp.int32, (half, half), 0)
    col = lax.broadcasted_iota(jnp.int32, (half, half), 1)
    tail_row = lax.broadcasted_iota(jnp.int32, (tail, size), 0)

    def schur(n, carry):
        total = d_ref[n]
        for k in range(3):
            t = target_ref[3 * n + k]
            c = rank_ref[3 * n + k]
            packed = near_ref[t, pl.ds(pl.multiple_of(c * half, half), half), :]
            packed = packed.astype(jnp.float32)
            tile = near_ref[t, pl.ds(capacity * half, tail), :].astype(jnp.float32)
            diag = jnp.sum(jnp.where(tail_row == c, tile, 0.0), axis=0, keepdims=True)
            flipped = packed.T
            part = packed[:, :half]
            part_t = flipped[:half, :]
            first = jnp.where(row >= col, part, part_t)
            last = jnp.where(row < col, part, part_t)
            last = jnp.where(row == col, diag[:, half:], last)
            inverse = jnp.concatenate(
                [joined(first, packed[:, half:]), joined(flipped[half:, :], last)], axis=0
            ).astype(jnp.bfloat16)
            coupling = c_ref[n, k]
            f = dot_nn(coupling, inverse) * scale
            high, low = split2(f)
            fh_ref[n, k] = high
            fl_ref[n, k] = low
            total = total - scale * dot_nt(joined(high, low), joined(coupling, coupling))
        m[pl.ds(pl.multiple_of(n * size, size), size), :] = total
        return carry

    lax.fori_loop(0, count, schur, 0, unroll=7)
    for n in range(count, pad):
        m[pl.ds(n * size, size), :] = d_ref[0]
    eliminate(m, pscr, qscr, count, pad, size)
    out_ref[...] = jnp.zeros_like(out_ref)
    for n in range(count):
        k = m[pl.ds(n * size, size), :]
        k_ref[n] = k
        kh, kl = split2(k)
        vh, vl = split2(v_ref[:, n * size : (n + 1) * size])
        left = dot_nn(joined(vh, vh, vl), jnp.concatenate([kh, kl, kh], axis=0))
        left_ref[n] = left
        lh, ll = split2(left)
        for k in range(3):
            r = 3 * n + k
            fh, fl = fh_ref[n, k], fl_ref[n, k]
            sent = dot_nn(joined(lh, lh, ll), jnp.concatenate([fh, fl, fh], axis=0))
            out_ref[target_ref[r] * capacity + rank_ref[r]] = (-sent).astype(out_ref.dtype)


def add_arrived(total, incoming_ref, get, slots):
    count = total.shape[0] - 1
    for s in range(slots):
        wanted = incoming_ref[s]
        spot = jnp.where(wanted < 0, count, wanted)
        total[spot] = total[spot] + get(s).astype(jnp.float32)


def left_kernel(
    capacity, scale, target_ref, rank_ref, incoming_ref, arrived_ref, left_in, c_ref,
    left_ref, out_ref, total,
):
    count = left_in.shape[0]
    slots = arrived_ref.shape[0]
    total[:count] = left_in[...]
    total[count] = jnp.zeros_like(total[count])
    add_arrived(total, incoming_ref, lambda s: arrived_ref[s], slots)
    left_ref[...] = total[:count]
    for s in range(slots):
        spot = s // capacity * 2 * capacity + s % capacity
        out_ref[spot] = total[jnp.maximum(incoming_ref[s], 0)].astype(out_ref.dtype)
        out_ref[spot + capacity] = jnp.zeros_like(out_ref[spot + capacity])
    for n in range(count):
        lh, ll = split2(total[n])
        both = joined(lh, ll)
        for k in range(3):
            r = 3 * n + k
            coupling = c_ref[n, k]
            sent = scale * dot_nn(both, jnp.concatenate([coupling, coupling], axis=0))
            spot = target_ref[r] * (2 * capacity) + capacity + rank_ref[r]
            out_ref[spot] = sent.astype(out_ref.dtype)


def middle_kernel(
    capacity, scale, target_ref, rank_ref, incoming_ref, arrived_ref, own_ref, c_ref,
    middle_ref, out_ref, total,
):
    count = own_ref.shape[0]
    slots = out_ref.shape[0]
    total[count] = jnp.zeros_like(total[count])
    for n in range(count):
        near = own_ref[n]
        for k in range(3):
            r = 3 * n + k
            got = arrived_ref[target_ref[r] * (2 * capacity) + rank_ref[r]]
            near = near + scale * dot_nt(got, c_ref[n, k])
        total[n] = near
    add_arrived(
        total,
        incoming_ref,
        lambda s: arrived_ref[s // capacity * 2 * capacity + capacity + s % capacity],
        slots,
    )
    middle_ref[...] = total[:count]
    for s in range(slots):
        out_ref[s] = total[jnp.maximum(incoming_ref[s], 0)].astype(out_ref.dtype)


def final_kernel(
    capacity, target_ref, rank_ref, arrived_ref, middle_ref, k_ref, fh_ref, fl_ref, out_ref
):
    count, size, _ = k_ref.shape
    for n in range(count):
        part = middle_ref[n]
        for k in range(3):
            r = 3 * n + k
            got = arrived_ref[target_ref[r] * capacity + rank_ref[r]]
            part = part - dot_nt(joined(got, got), joined(fh_ref[n, k], fl_ref[n, k]))
        ph, plow = split2(part)
        kh, kl = split2(k_ref[n])
        out_ref[:, n * size : (n + 1) * size] = dot_nt(
            joined(ph, ph, plow), joined(kh, kl, kh)
        )


def call(kernel, scalars, arrays, shapes, scratch=()):
    smem = pl.BlockSpec(memory_space=pltpu.SMEM)
    vmem = pl.BlockSpec(memory_space=pltpu.VMEM)
    return pl.pallas_call(
        kernel,
        out_shape=[jax.ShapeDtypeStruct(shape, dtype) for shape, dtype in shapes],
        in_specs=[smem] * len(scalars) + [vmem] * len(arrays),
        out_specs=[vmem] * len(shapes),
        scratch_shapes=[pltpu.VMEM(shape, jnp.float32) for shape in scratch],
    )(*scalars, *arrays)


def build_diag(noise_block, shift_block, factor):
    noise_block = noise_block.astype(jnp.float32) * factor
    symmetric = (noise_block + jnp.swapaxes(noise_block, -1, -2)) * 0.5
    eye_block = jnp.eye(noise_block.shape[-1], dtype=jnp.float32)
    return symmetric + shift_block.astype(jnp.float32)[..., :, None] * eye_block


def exchange(x, dev_count):
    shape = x.shape
    x = x.reshape(dev_count, -1, *shape[1:])
    x = lax.all_to_all(x, "rows", split_axis=0, concat_axis=0, tiled=True)
    return x.reshape(shape)


def body(diag_noise, couplings, shifts, near_devices, near_slots, vectors):
    dev_count = lax.axis_size("rows")
    my_index = lax.axis_index("rows")
    row_count = diag_noise.shape[0]
    block_size = diag_noise.shape[1]
    vec_count = vectors.shape[0]
    capacity = 3 * row_count // (dev_count - 1) + 2
    slot_total = dev_count * capacity
    factor = 0.5 / math.sqrt(block_size)
    coupling_factor = 0.4 / math.sqrt(block_size)
    target = ((my_index - 1 - near_devices) % dev_count).reshape(-1)
    device_onehot = (target[:, None] == jnp.arange(dev_count, dtype=jnp.int32)[None, :]).astype(
        jnp.int32
    )
    running = jnp.cumsum(device_onehot, axis=0) - 1
    rank = jnp.sum(running * device_onehot, axis=1)
    position = target * capacity + rank
    hit = position[None, :] == jnp.arange(slot_total, dtype=jnp.int32)[:, None]
    asked_slots = jnp.sum(jnp.where(hit, near_slots.reshape(1, -1) + 1, 0), axis=1) - 1
    incoming = exchange(asked_slots, dev_count)
    served = jnp.maximum(incoming, 0)
    diag_own = build_diag(diag_noise, shifts, factor)

    bf16, f32 = jnp.bfloat16, jnp.float32
    half = block_size // 2
    tail = 16
    pad = -(-row_count // 8) * 8
    work = ((pad * block_size, block_size),) + ((PANEL * pad, block_size),) * 2
    packed, diags = call(
        inverse_kernel,
        (),
        (diag_own,),
        (((row_count, half, block_size), bf16), ((row_count, tail, block_size), bf16)),
        work,
    )
    (answer,) = call(
        functools.partial(answer_kernel, capacity),
        (served,),
        (packed, diags),
        (((dev_count, capacity * half + tail, block_size), bf16),),
    )
    near = exchange(answer, dev_count)
    rows_shape = (row_count, vec_count, block_size)
    total_shape = ((row_count + 1, vec_count, block_size),)
    slots_shape = (slot_total, vec_count, block_size)
    f_shape = (row_count, 3, block_size, block_size)
    k_all, f_high, f_low, left, outgoing = call(
        functools.partial(factor_kernel, capacity, coupling_factor),
        (target, rank),
        (near, couplings, diag_own, vectors),
        (
            ((row_count, block_size, block_size), f32),
            (f_shape, bf16),
            (f_shape, bf16),
            (rows_shape, f32),
            (slots_shape, bf16),
        ),
        work,
    )
    arrived = exchange(outgoing, dev_count)
    left, outgoing = call(
        functools.partial(left_kernel, capacity, coupling_factor),
        (target, rank, incoming),
        (arrived, left, couplings),
        ((rows_shape, f32), ((2 * slot_total, vec_count, block_size), bf16)),
        total_shape,
    )
    arrived = exchange(outgoing, dev_count)
    own = jnp.einsum("rva,rab->rvb", left, diag_own, precision=highest)
    middle, outgoing = call(
        functools.partial(middle_kernel, capacity, coupling_factor),
        (target, rank, incoming),
        (arrived, own, couplings),
        ((rows_shape, f32), (slots_shape, bf16)),
        total_shape,
    )
    arrived = exchange(outgoing, dev_count)
    (result,) = call(
        functools.partial(final_kernel, capacity),
        (target, rank),
        (arrived, middle, k_all, f_high, f_low),
        ((vectors.shape, f32),),
    )
    return result


def solution(mesh):
    return jax.shard_map(
        body,
        mesh=mesh,
        in_specs=(
            P("rows", None, None),
            P("rows", None, None, None),
            P("rows", None),
            P("rows", None),
            P("rows", None),
            P(None, "rows"),
        ),
        out_specs=P(None, "rows"),
        check_vma=False,
    )
```
